32 devices in a mesh: dp: 4 (over y, x), expert: 8 (over z, core).
Axes of the slice: x: 2, y: 2, z: 4, core: 2. Of those that a mesh axis runs over, the one named last changes fastest.
Arguments:
- tokens: bfloat16 [2, 2048, 4096], P(None, ('dp', 'expert')), may hold values from -64 to 64
- expert_of: int32 [2, 2048], P(None, ('dp', 'expert')), may hold values from 0 to 3, as said below
- w_gate: bfloat16 [8, 4096, 3584], P('expert', None, 'dp'), may hold values from -0.09375 to 0.09375
- w_up: bfloat16 [8, 4096, 3584], P('expert', None, 'dp'), may hold values from -0.09375 to 0.09375
- w_down: bfloat16 [8, 3584, 4096], P('expert', 'dp'), may hold values from -1 to 1
Outputs:
- out: bfloat16 [2, 2048, 4096], P(None, ('dp', 'expert'))
- next_scale: float32 [4], replicated
The draws below stay inside these ranges and needn't reach their ends.
Inputs may be any that keep to these rules, and one draw needn't show every extreme that they name: `expert_of`: in each microbatch the 64 tokens of one device name each expert at most 18 times, and one expert, the same for all devices of that microbatch, exactly 18 times.
All inputs are finite; a program needn't handle non-finite values.
Results may differ from the reference program's by a relative error of at most 0.012.
Values may be sent and summed in bfloat16 or wider, within the bound.
A program may use at most 128 MiB of HBM per device.

```python
import math
import jax
import jax.numpy as jnp
from jax import lax

D = 4096
FF = 7168
SPAN = 2
MICRO = 2
TOK_DEV = 64
EXPERTS = 4
CAP = 18
TOKENS = 2048
N_DP = 4


def draw_tokens(key, part):
    keys_all = jax.random.split(jax.random.fold_in(key, 3), 4)
    shape_all = (MICRO, TOKENS, D)
    base_values = jnp.clip(jax.random.normal(keys_all[0], shape_all, jnp.float32), -5.5, 5.5)
    row_scale = jnp.exp(jax.random.uniform(keys_all[2], (MICRO, TOKENS, 1), jnp.float32, math.log(0.2), math.log(2.0)))
    rising = jnp.exp(0.5 * math.log(3.0) * jnp.arange(TOKENS, dtype=jnp.float32) / max(TOKENS - 1, 1))[None, :, None]
    column_scale = jnp.exp(jax.random.uniform(keys_all[3], (1, 1, D), jnp.float32, math.log(0.32), math.log(3.2)))
    return (base_values * row_scale * rising * column_scale).astype(jnp.bfloat16)


def draw_w_down(key, part):
    keys_all = jax.random.split(jax.random.fold_in(key, 5), 2)
    shape_all = (EXPERTS, SPAN, FF // SPAN, D)
    base_values = jnp.clip(jax.random.normal(keys_all[0], shape_all, jnp.float32), -6.0, 6.0)
    ladder = jnp.arange(EXPERTS, dtype=jnp.float32) / max(EXPERTS - 1, 1)
    gain_ladder = jnp.exp(math.log(0.25) + ladder * (math.log(2.5) - math.log(0.25)))
    expert_gain = jax.random.permutation(keys_all[1], gain_ladder).reshape(EXPERTS, 1, 1, 1)
    weights = base_values * expert_gain * FF ** (-0.5)
    return weights.reshape(EXPERTS * SPAN, FF // SPAN, D).astype(jnp.bfloat16)


def draw_expert_of(key, part):
    blocks = TOKENS // TOK_DEV

    def one_block(block_key, full_expert):
        first_key, second_key = jax.random.split(block_key)
        others = jnp.arange(EXPERTS - 1, dtype=jnp.int32)
        others = jnp.where(others >= full_expert, others + 1, others).astype(jnp.int32)
        slot_pool = jnp.repeat(others, CAP)
        chosen = jax.random.permutation(first_key, slot_pool)[:TOK_DEV - CAP]
        block_ids = jnp.concatenate([jnp.full((CAP,), full_expert, jnp.int32), chosen.astype(jnp.int32)])
        return jax.random.permutation(second_key, block_ids)

    def one_micro(micro_key):
        full_key, block_key = jax.random.split(micro_key)
        full_expert = jax.random.randint(full_key, (), 0, EXPERTS, dtype=jnp.int32)
        block_keys = jax.random.split(block_key, blocks)
        return jax.vmap(lambda single_key: one_block(single_key, full_expert))(block_keys)
    micro_keys = jax.random.split(jax.random.fold_in(key, 11), MICRO)
    return jax.vmap(one_micro)(micro_keys).reshape(MICRO, TOKENS).astype(jnp.int32)


def block_scale(rng, extent, cuts, least, largest):
    factor_of = 1.0
    for axis_at, blocks in cuts:
        heights = jax.random.uniform(jax.random.fold_in(jax.random.fold_in(rng, 6), axis_at), (blocks,), jnp.float32, least / len(cuts), largest / len(cuts))
        factor_of = factor_of * jnp.repeat(jnp.exp(heights), extent[axis_at] // blocks).reshape((-1,) + (1,) * (len(extent) - 1 - axis_at))
    return factor_of


def scatter_about(own_key, shape, deviation, bound, cuts=(), held_as=jnp.bfloat16):
    entries = deviation * jax.random.normal(own_key, shape, jnp.float32)
    if cuts:
        entries = entries * block_scale(own_key, shape, cuts, -0.22, 0.18)
    return jnp.clip(entries, -bound, bound).astype(held_as)


def setup_inputs(seed: int = 0) -> dict:
    arg_keys = jax.random.split(jax.random.key(seed), 6)
    return {
        "tokens": draw_tokens(jax.random.fold_in(arg_keys[5], 71), 0),
        "expert_of": draw_expert_of(jax.random.fold_in(arg_keys[5], 71), 0),
        "w_gate": scatter_about(arg_keys[2], (EXPERTS * SPAN, D, FF // SPAN), D ** -0.5, 0.09375, ((0, 8), (2, 4))),
        "w_up": scatter_about(arg_keys[3], (EXPERTS * SPAN, D, FF // SPAN), D ** -0.5, 0.09375, ((0, 8), (2, 4))),
        "w_down": draw_w_down(jax.random.fold_in(arg_keys[5], 71), 0),
    }


clip_target = 2.0

def block_slots(block_ids):
    onehot_ids = (block_ids[:, None] == jnp.arange(EXPERTS, dtype=jnp.int32)[None, :]).astype(jnp.int32)
    earlier = jnp.cumsum(onehot_ids, axis=0) - onehot_ids
    return lax.optimization_barrier(jnp.sum(earlier * onehot_ids, axis=1)).astype(jnp.int32)

def expert_rows(operands):
    rows_in, gate_rows, up_rows, down_rows = operands
    group_width = FF // (SPAN * N_DP)
    total_out = jnp.zeros((rows_in.shape[0], D), jnp.float32)
    for half_idx in range(SPAN):
        summed = jnp.zeros((rows_in.shape[0], D), jnp.float32)
        for quarter in range(N_DP):
            low_col = quarter * group_width
            gate_vals = jnp.dot(rows_in, gate_rows[half_idx, :, low_col:low_col + group_width], preferred_element_type=jnp.float32)
            up_vals = jnp.dot(rows_in, up_rows[half_idx, :, low_col:low_col + group_width], preferred_element_type=jnp.float32)
            hidden = (jax.nn.silu(gate_vals) * up_vals).astype(jnp.bfloat16)
            part_out = jnp.dot(hidden, down_rows[half_idx, low_col:low_col + group_width, :], preferred_element_type=jnp.float32)
            part_out = lax.optimization_barrier(part_out.astype(jnp.bfloat16))
            summed = summed + part_out.astype(jnp.float32)
        half_out = lax.optimization_barrier(summed.astype(jnp.bfloat16))
        total_out = total_out + half_out.astype(jnp.float32)
    return total_out

def reference(tokens, expert_of, w_gate, w_up, w_down):
    blocks = TOKENS // TOK_DEV
    gate_all = w_gate.reshape(EXPERTS, SPAN, D, FF // SPAN)
    up_all = w_up.reshape(EXPERTS, SPAN, D, FF // SPAN)
    down_all = w_down.reshape(EXPERTS, SPAN, FF // SPAN, D)
    clip_scale = jnp.ones((EXPERTS,), jnp.float32)
    outputs = []
    for micro_idx in range(MICRO):
        token_ids = expert_of[micro_idx].astype(jnp.int32)
        slot_of = jax.vmap(block_slots)(token_ids.reshape(blocks, TOK_DEV)).reshape(TOKENS)
        block_of = (jnp.arange(TOKENS, dtype=jnp.int32) // TOK_DEV).astype(jnp.int32)
        gated = (clip_scale[token_ids][:, None] * tokens[micro_idx].astype(jnp.float32)).astype(jnp.bfloat16)
        position = ((token_ids * blocks + block_of) * CAP + slot_of).astype(jnp.int32)
        dispatched = jnp.zeros((EXPERTS * blocks * CAP, D), jnp.bfloat16).at[position].set(gated)
        dispatched = dispatched.reshape(EXPERTS, blocks * CAP, D)
        expert_out = lax.map(expert_rows, (dispatched, gate_all, up_all, down_all))
        token_out = expert_out.reshape(EXPERTS * blocks * CAP, D)[position]
        outputs.append(token_out.astype(jnp.bfloat16))
        squares = lax.optimization_barrier(jnp.sum(token_out * token_out, axis=1))
        counts = jax.ops.segment_sum(jnp.ones((TOKENS,), jnp.float32), token_ids, EXPERTS)
        square_sums = jax.ops.segment_sum(squares, token_ids, EXPERTS)
        clip_scale = jnp.minimum(1.0, clip_target / jnp.sqrt((square_sums + D) / (D * (counts + 1.0))))
    return (jnp.stack(outputs), clip_scale)
```

```python
import functools

import jax
import jax.numpy as jnp
from jax import lax
from jax.experimental import pallas as pl
from jax.experimental.pallas import tpu as pltpu
from jax.sharding import PartitionSpec as P

SPAN = 2


clip_target = 2.0


def body(tokens, expert_of, w_gate, w_up, w_down):
    micro_count = tokens.shape[0]
    tok_rows = tokens.shape[1]
    model_width = tokens.shape[2]
    expert_size = lax.axis_size("expert")
    expert_count = expert_size // SPAN
    capacity = max(2, 9 * tok_rows // (8 * expert_count))
    my_expert = lax.axis_index("expert") // SPAN
    gate_local = w_gate[0]
    up_local = w_up[0]
    down_local = w_down[0]
    slot_range = jnp.arange(expert_count * capacity, dtype=jnp.int32)
    expert_range = jnp.arange(expert_count, dtype=jnp.int32)
    clip_scale = jnp.ones((expert_count,), jnp.float32)
    results = []
    for micro_idx in range(micro_count):
        token_ids = expert_of[micro_idx]
        onehot_ids = (token_ids[:, None] == expert_range[None, :]).astype(jnp.int32)
        earlier = jnp.cumsum(onehot_ids, axis=0) - onehot_ids
        slot_of = jnp.sum(earlier * onehot_ids, axis=1)
        position = token_ids * capacity + slot_of
        placing = (position[None, :] == slot_range[:, None]).astype(jnp.bfloat16)
        tokens_now = tokens[micro_idx]
        packed = jnp.dot(placing, tokens_now, preferred_element_type=jnp.float32).astype(
            jnp.bfloat16
        )
        packed = packed.reshape(expert_count, capacity, model_width)
        factor = clip_scale[my_expert]
        sending_all = jnp.repeat(packed, SPAN, axis=0)
        arrived = lax.all_to_all(sending_all, "expert", split_axis=0, concat_axis=0, tiled=True)
        flat_rows = arrived.reshape(expert_size * capacity, model_width)
        rows_in = lax.all_gather(flat_rows, "dp", axis=0, tiled=True)
        rows_in = (factor * rows_in.astype(jnp.float32)).astype(jnp.bfloat16)
        gate_vals = jnp.dot(rows_in, gate_local, preferred_element_type=jnp.float32)
        up_vals = jnp.dot(rows_in, up_local, preferred_element_type=jnp.float32)
        hidden = (jax.nn.silu(gate_vals) * up_vals).astype(jnp.bfloat16)
        summed = lax.psum_scatter(
            jnp.dot(hidden, down_local, preferred_element_type=jnp.float32).astype(jnp.bfloat16),
            "dp",
            scatter_dimension=0,
            tiled=True,
        )
        halves = summed.reshape(expert_size, capacity, model_width)
        returned = lax.all_to_all(halves, "expert", split_axis=0, concat_axis=0, tiled=True)
        returned = lax.optimization_barrier(returned)
        joined = jnp.sum(
            returned.reshape(expert_count, SPAN, capacity, model_width).astype(jnp.float32), axis=1
        )
        token_out = jnp.take(joined.reshape(expert_count * capacity, model_width), position, axis=0)
        results.append(token_out.astype(jnp.bfloat16))
        squares = jnp.sum(token_out * token_out, axis=1)
        onehot_float = onehot_ids.astype(jnp.float32)
        counts_local = jnp.sum(onehot_float, axis=0)
        square_local = jnp.dot(squares[None, :], onehot_float, precision=lax.Precision.HIGHEST)[0]
        counts, square_sums = lax.psum((counts_local, square_local), ("dp", "expert"))
        clip_scale = jnp.minimum(
            1.0,
            clip_target / jnp.sqrt((square_sums + model_width) / (model_width * (counts + 1.0))),
        )
    return (jnp.stack(results), clip_scale)


MESH = pl.DeviceIdType.MESH
F32 = jnp.float32
BF16 = jnp.bfloat16
ROWS = 16
CHUNKS = 4
LANES = 128


def mm(a, b):
    return jnp.dot(a, b, preferred_element_type=F32)


def iota(shape, dim):
    return lax.broadcasted_iota(jnp.int32, shape, dim)


def kernel(
    sizes,
    tok_ref, idr_ref, idc_ref, wg_hbm, wu_hbm, wd_hbm,
    out_ref, scale_ref,
    wg, wu, wd, pk, xg, xr, hid, g1, u1, sb, rb, own, rd, ra, rc, fr, f2, ret,
    cst, sqst, fst,
    wsem, ssem, rsem, lsem, csend, crecv, qsend, qrecv, fsend, frecv,
):
    micro, toks, width, ff, nd, ne, cap = sizes
    extra = cap - ROWS
    pieces = ROWS // extra
    piece = width // pieces
    experts = ne // SPAN
    blocks = experts * SPAN
    main_rows = blocks * ROWS
    extra_rows = blocks * extra
    half = width // 2
    ch = half // CHUNKS
    pair_w = 2 * ch
    pair_piece = pair_w // pieces
    ndev = nd * ne

    d = lax.axis_index("dp")
    ex = lax.axis_index("expert")
    z = ex // 2
    c = ex % 2
    dx = d + 1 - 2 * (d % 2)
    dy = d + 2 - 4 * (d // 2)
    dd = 3 - d
    sib = z * 2 + 1 - c
    flat = d * ne + ex
    flat_q = d * 2 + c

    weights = [
        pltpu.make_async_copy(wg_hbm.at[0], wg, wsem.at[0]),
        pltpu.make_async_copy(wu_hbm.at[0], wu, wsem.at[1]),
        pltpu.make_async_copy(wd_hbm.at[0], wd, wsem.at[2]),
    ]
    for copy in weights:
        copy.start()

    barrier = pltpu.get_barrier_semaphore()

    def greet(t, carry):
        to = (flat + t) % ndev
        pl.semaphore_signal(barrier, inc=1, device_id=(to // ne, to % ne), device_id_type=MESH)
        return carry

    lax.fori_loop(1, ndev, greet, 0)

    slots = experts * ROWS
    place = []
    counts = []
    for m in range(micro):
        idr = idr_ref[m]
        idc = idc_ref[m]
        before_r = (idc == idr) & (iota((toks, toks), 0) < iota((toks, toks), 1))
        slot_r = jnp.sum(before_r.astype(F32), axis=0, keepdims=True).astype(jnp.int32)
        before_c = (idc == idr) & (iota((toks, toks), 1) < iota((toks, toks), 0))
        slot_c = jnp.sum(before_c.astype(F32), axis=1, keepdims=True).astype(jnp.int32)
        place.append((idr, idc, slot_r, slot_c))
        hit = (idc == iota((toks, LANES), 1)).astype(F32)
        counts.append(jnp.sum(hit, axis=0, keepdims=True))
    row8 = iota((8, LANES), 0)
    lane8 = iota((8, LANES), 1)
    count_tile = jnp.zeros((8, LANES), F32)
    for m in range(micro):
        count_tile = jnp.where(row8 == m, counts[m], count_tile)
    cst[flat] = count_tile

    def pack(m):
        idr, _, slot_r, _ = place[m]
        row = iota((slots, toks), 0)
        pick = ((idr == row // ROWS) & (slot_r == row % ROWS)).astype(F32).astype(BF16)
        pick_x = ((idr == row // ROWS) & (slot_r == ROWS + (row % ROWS) // pieces)).astype(F32).astype(BF16)
        rowp = iota((slots, piece), 0) % pieces
        tail = jnp.zeros((slots, piece), F32)
        for p in range(pieces):
            cols = tok_ref[m, :, p * piece:(p + 1) * piece]
            pk[m, :, :, p * piece:(p + 1) * piece] = mm(pick, cols).astype(BF16).reshape(experts, ROWS, piece)
            tail = jnp.where(rowp == p, mm(pick_x, cols), tail)
        pk[m, :, :, width:] = tail.astype(BF16).reshape(experts, ROWS, piece)

    sends = []
    index = {}

    def sem_of(key):
        return index.setdefault(key, len(index))

    def remote(key, src, dst, dev):
        i = sem_of(key)
        copy = pltpu.make_async_remote_copy(
            src_ref=src, dst_ref=dst, send_sem=ssem.at[i], recv_sem=rsem.at[i],
            device_id=dev, device_id_type=MESH,
        )
        copy.start()
        sends.append((key, copy))
        return copy

    def arrived(key, dst):
        i = sem_of(key)
        pltpu.make_async_remote_copy(
            src_ref=dst, dst_ref=dst, send_sem=ssem.at[i], recv_sem=rsem.at[i],
            device_id=(d, sib), device_id_type=MESH,
        ).wait_recv()

    def wait_sent(match):
        left = []
        for key, copy in sends:
            if match(key):
                copy.wait_send()
            else:
                left.append((key, copy))
        sends[:] = left

    locals_ = {}

    def local(key, src, dst):
        i = len(locals_)
        copy = pltpu.make_async_copy(src, dst, lsem.at[i])
        copy.start()
        locals_[key] = copy

    def zof(t):
        return (z + experts - t) % experts

    def dispatch(m):
        local(("z", m), pk.at[m, z], xg.at[m, d, c * experts + z])
        for t in range(1, experts):
            to = (z + t) % experts
            remote(("z", m, t), pk.at[m, to], xg.at[m, d, c * experts + z], (d, to * 2 + c))

    def to_sibling(kind, m, t, slot):
        remote(("s" + kind, m, t), slot, slot, (d, sib))

    def gather_own(m, t):
        slot = xg.at[m, d, c * experts + zof(t)]
        if t == 0:
            locals_[("z", m)].wait()
        else:
            arrived(("z", m, t), slot)
        remote(("gx", m, t), slot, slot, (dx, ex))
        remote(("gy", m, t), slot, slot, (dy, ex))
        to_sibling("o", m, t, slot)

    def gather_xy(m, t):
        slot = xg.at[m, dx, c * experts + zof(t)]
        arrived(("gx", m, t), slot)
        if t < experts // 2:
            remote(("gd", m, t), slot, slot, (dy, ex))
        to_sibling("x", m, t, slot)
        slot = xg.at[m, dy, c * experts + zof(t)]
        arrived(("gy", m, t), slot)
        if t >= experts // 2:
            remote(("gd", m, t), slot, slot, (dx, ex))
        to_sibling("y", m, t, slot)

    def gather_diag(m, t):
        slot = xg.at[m, dd, c * experts + zof(t)]
        arrived(("gd", m, t), slot)
        to_sibling("d", m, t, slot)

    def gather_end(m):
        for kind, chip in (("o", d), ("x", dx), ("y", dy), ("d", dd)):
            for t in range(experts):
                arrived(("s" + kind, m, t), xg.at[m, chip, (1 - c) * experts + zof(t)])

    allm = nd * main_rows
    allx = nd * extra_rows

    def spread(m):
        def one(p, carry):
            row = iota((allx, allm), 0)
            want = (row // extra) * ROWS + (row % extra) * pieces + p
            pick = (iota((allx, allm), 1) == want).astype(F32).astype(BF16)
            tails = xg[m, :, :, :, width:].reshape(allm, piece)
            xr[:, pl.ds(pl.multiple_of(p * piece, piece), piece)] = mm(pick, tails).astype(BF16)
            return carry

        lax.fori_loop(0, pieces, one, 0)

    def gate_up(m, low, high):
        def one(n, carry):
            cols = pl.ds(pl.multiple_of(n * LANES, LANES), LANES)
            rows = jnp.concatenate([xg[m, :, :, :, :width].reshape(allm, width), xr[...]], axis=0)
            w = jnp.concatenate([wg[:, cols], wu[:, cols]], axis=1)
            both = mm(rows, w)
            gate = both[:, :LANES]
            up = both[:, LANES:]
            if m == 0:
                hid[:, cols] = (gate / (1.0 + jnp.exp(-gate)) * up).astype(BF16)
            else:
                g1[:, cols] = gate
                u1[:, cols] = up
            return carry

        lax.fori_loop(low, high, one, 0)

    def scaled_hidden(scale):
        def one(n, carry):
            cols = pl.ds(pl.multiple_of(n * LANES, LANES), LANES)
            gate = g1[:, cols] * scale
            up = u1[:, cols] * scale
            hid[:, cols] = (gate / (1.0 + jnp.exp(-gate)) * up).astype(BF16)
            return carry

        lax.fori_loop(0, ff // LANES, one, 0)

    def neighbours(j):
        return (dx, dy) if j % 2 == 0 else (dy, dx)

    def down(side, j):
        col = pl.multiple_of(side * half + j * ch, ch)
        return mm(hid[...], wd[:, pl.ds(col, ch)])

    def step_a(m, j):
        if m > 0:
            wait_sent(lambda key: key == ("rs", m - 1, j))
        sb[j] = down(1 - c, j).astype(BF16)
        remote(("rs", m, j), sb.at[j], rb.at[m, j], (d, sib))

    def step_b(m, j):
        mine = down(c, j)
        if m > 0:
            wait_sent(lambda key: key[0] in ("rd", "ra", "rc") and key[1:] == (m - 1, j))
        arrived(("rs", m, j), rb.at[m, j])
        both = (mine + rb[m, j].astype(F32)).astype(BF16)
        for k in range(nd):
            own[j, k, :main_rows] = both[k * main_rows:(k + 1) * main_rows]
            own[j, k, main_rows:] = both[allm + k * extra_rows:allm + (k + 1) * extra_rows]
        first, _ = neighbours(j)
        remote(("rd", m, j), own.at[j, dd], rd.at[m, j], (first, ex))
        remote(("ra", m, j), own.at[j, first], ra.at[m, j], (first, ex))

    def step_c(m, j):
        _, second = neighbours(j)
        arrived(("rd", m, j), rd.at[m, j])
        own[j, second] = (own[j, second].astype(F32) + rd[m, j].astype(F32)).astype(BF16)
        remote(("rc", m, j), own.at[j, second], rc.at[m, j], (second, ex))

    def step_d(m, j):
        arrived(("ra", m, j), ra.at[m, j])
        arrived(("rc", m, j), rc.at[m, j])
        total = own[j, d].astype(F32) + ra[m, j].astype(F32) + rc[m, j].astype(F32)
        at = (j % 2) * ch
        pair = j // 2
        low = total.astype(BF16)
        f2[m, pair, :, :, at:at + ch] = low[:main_rows].reshape(blocks, ROWS, ch)
        fr[:, at:at + ch] = low[main_rows:]
        if j % 2 == 1:
            row = iota((main_rows, extra_rows), 0)
            want = (row // ROWS) * extra + (row % ROWS) // pieces
            pick = (iota((main_rows, extra_rows), 1) == want).astype(F32).astype(BF16)
            rowp = iota((main_rows, pair_piece), 0) % pieces
            tail = jnp.zeros((main_rows, pair_piece), F32)
            for p in range(pieces):
                tail = jnp.where(rowp == p, mm(pick, fr[:, p * pair_piece:(p + 1) * pair_piece]), tail)
            f2[m, pair, :, :, pair_w:] = tail.astype(BF16).reshape(blocks, ROWS, pair_piece)
            local(("f", m, pair), f2.at[m, pair, c * experts + z], ret.at[m, z, c, pair])
            for t in range(1, blocks):
                to = (ex + t) % blocks
                remote(
                    ("f", m, pair, t), f2.at[m, pair, (to % 2) * experts + to // 2],
                    ret.at[m, z, c, pair], (d, to),
                )
        return jnp.sum(jnp.sum(total * total, axis=0, keepdims=True), axis=1, keepdims=True)

    def unpack(m):
        _, idc, _, slot_c = place[m]
        col = iota((toks, slots), 1)
        pick = ((idc == col // ROWS) & (slot_c == col % ROWS)).astype(F32).astype(BF16)
        pick_x = (idc == col // ROWS) & (slot_c == ROWS + (col % ROWS) // pieces)
        for pair in range(CHUNKS // 2):
            locals_[("f", m, pair)].wait()
            for t in range(1, blocks):
                frm = (ex + blocks - t) % blocks
                arrived(("f", m, pair, t), ret.at[m, frm // 2, frm % 2, pair])
        for h in range(2):
            for pair in range(CHUNKS // 2):
                for p in range(pieces):
                    at = p * pair_piece
                    main = ret[m, :, h, pair, :, at:at + pair_piece].reshape(slots, pair_piece)
                    tails = ret[m, :, h, pair, :, pair_w:].reshape(slots, pair_piece)
                    pick_p = (pick_x & (col % pieces == p)).astype(F32).astype(BF16)
                    value = mm(pick, main) + mm(pick_p, tails)
                    base = h * half + pair * pair_w + at
                    out_ref[m, :, base:base + pair_piece] = value.astype(BF16)

    def clip(total, count):
        return jnp.minimum(1.0, clip_target / jnp.sqrt((total + width) / (width * (count + 1.0))))

    pack(0)
    pl.semaphore_wait(barrier, ndev - 1)
    dispatch(0)
    pack(1)
    dispatch(1)

    def spread_stats(buf, me, peers, ssems, rsems, dev_of):
        def one(t, carry):
            pltpu.make_async_remote_copy(
                src_ref=buf.at[me], dst_ref=buf.at[me], send_sem=ssems.at[t], recv_sem=rsems.at[t],
                device_id=dev_of((me + t) % peers), device_id_type=MESH,
            ).start()
            return carry

        lax.fori_loop(1, peers, one, 0)

    def await_stats(buf, me, peers, ssems, rsems, dev_of):
        def one(t, carry):
            frm = (me + peers - t) % peers
            copy = pltpu.make_async_remote_copy(
                src_ref=buf.at[me], dst_ref=buf.at[frm], send_sem=ssems.at[t], recv_sem=rsems.at[t],
                device_id=dev_of((me + t) % peers), device_id_type=MESH,
            )
            copy.wait_recv()
            copy.wait_send()
            return carry

        lax.fori_loop(1, peers, one, 0)

    whole = (ndev, csend, crecv, lambda g: (g // ne, g % ne))
    plane = (nd * 2, qsend, qrecv, lambda q: (q // 2, z * 2 + q % 2))
    last = (ndev, fsend, frecv, lambda g: (g // ne, g % ne))

    spread_stats(cst, flat, *whole)
    for t in range(experts):
        gather_own(0, t)
    for t in range(experts):
        gather_xy(0, t)
    for t in range(experts):
        gather_diag(0, t)
    gather_end(0)
    weights[0].wait()
    weights[1].wait()
    tiles = ff // LANES
    marks = [0, (2 * tiles) // 7, (4 * tiles) // 7, (6 * tiles) // 7, tiles]
    spread(0)
    gate_up(0, marks[0], marks[1])
    for t in range(experts):
        gather_own(1, t)
    gate_up(0, marks[1], marks[2])
    for t in range(experts // 2):
        gather_xy(1, t)
    gate_up(0, marks[2], marks[4])
    for t in range(experts // 2, experts):
        gather_xy(1, t)
    weights[2].wait()
    step_a(0, 0)
    step_a(0, 1)
    step_b(0, 0)
    step_a(0, 2)
    step_b(0, 1)
    step_a(0, 3)
    step_b(0, 2)
    step_b(0, 3)
    for t in range(experts):
        gather_diag(1, t)
    step_c(0, 0)
    step_c(0, 1)
    gather_end(1)
    spread(1)
    gate_up(1, marks[0], marks[2])
    step_c(0, 2)
    step_c(0, 3)
    squares = step_d(0, 0)
    squares = squares + step_d(0, 1)
    gate_up(1, marks[2], marks[4])
    squares = squares + step_d(0, 2)
    squares = squares + step_d(0, 3)
    sqst[flat_q] = jnp.broadcast_to(squares, (8, LANES))
    spread_stats(sqst, flat_q, *plane)
    await_stats(cst, flat, *whole)
    count_sum = jnp.sum(cst[...], axis=0)
    await_stats(sqst, flat_q, *plane)
    square_sum = jnp.sum(sqst[...], axis=0)[:1, :1]
    masked = jnp.where((row8 == 0) & (lane8 == z), count_sum, 0.0)
    count_here = jnp.sum(jnp.sum(masked, axis=0, keepdims=True), axis=1, keepdims=True)
    scaled_hidden(clip(square_sum, count_here))
    step_a(1, 0)
    step_a(1, 1)
    step_b(1, 0)
    step_a(1, 2)
    step_b(1, 1)
    step_c(1, 0)
    step_a(1, 3)
    step_b(1, 2)
    step_c(1, 1)
    step_b(1, 3)
    step_c(1, 2)
    squares = step_d(1, 0)
    step_c(1, 3)
    squares = squares + step_d(1, 1)
    unpack(0)
    squares = squares + step_d(1, 2)
    squares = squares + step_d(1, 3)
    fst[flat] = jnp.where(lane8 == z, jnp.broadcast_to(squares, (8, LANES)), 0.0)
    spread_stats(fst, flat, *last)
    unpack(1)
    await_stats(fst, flat, *last)
    count_last = jnp.sum(jnp.where(row8 == micro - 1, count_sum, 0.0), axis=0, keepdims=True)
    scale_ref[...] = clip(jnp.sum(fst[...], axis=0), count_last)
    wait_sent(lambda key: True)


def fused(sizes, tokens, expert_of, w_gate, w_up, w_down):
    micro, toks, width, ff, nd, ne, cap = sizes
    extra = cap - ROWS
    pieces = ROWS // extra
    piece = width // pieces
    experts = ne // SPAN
    blocks = experts * SPAN
    ch = width // 2 // CHUNKS
    wide = width + piece
    pair_wide = 2 * ch + 2 * ch // pieces
    rows = nd * blocks * cap
    one = blocks * cap
    ndev = nd * ne
    dma = pltpu.SemaphoreType.DMA
    vmem = pl.BlockSpec(memory_space=pltpu.VMEM)
    anyw = pl.BlockSpec(memory_space=pl.ANY)
    out, scale = pl.pallas_call(
        functools.partial(kernel, sizes),
        out_shape=(
            jax.ShapeDtypeStruct((micro, toks, width), BF16),
            jax.ShapeDtypeStruct((8, LANES), F32),
        ),
        in_specs=[vmem, vmem, vmem, anyw, anyw, anyw],
        out_specs=(vmem, vmem),
        scratch_shapes=[
            pltpu.VMEM((width, ff), BF16),
            pltpu.VMEM((width, ff), BF16),
            pltpu.VMEM((ff, width), BF16),
            pltpu.VMEM((micro, experts, ROWS, wide), BF16),
            pltpu.VMEM((micro, nd, blocks, ROWS, wide), BF16),
            pltpu.VMEM((nd * blocks * extra, width), BF16),
            pltpu.VMEM((rows, ff), BF16),
            pltpu.VMEM((rows, ff), F32),
            pltpu.VMEM((rows, ff), F32),
            pltpu.VMEM((CHUNKS, rows, ch), BF16),
            pltpu.VMEM((micro, CHUNKS, rows, ch), BF16),
            pltpu.VMEM((CHUNKS, nd, one, ch), BF16),
            pltpu.VMEM((micro, CHUNKS, one, ch), BF16),
            pltpu.VMEM((micro, CHUNKS, one, ch), BF16),
            pltpu.VMEM((micro, CHUNKS, one, ch), BF16),
            pltpu.VMEM((blocks * extra, 2 * ch), BF16),
            pltpu.VMEM((micro, CHUNKS // 2, blocks, ROWS, pair_wide), BF16),
            pltpu.VMEM((micro, experts, 2, CHUNKS // 2, ROWS, pair_wide), BF16),
            pltpu.VMEM((ndev, 8, LANES), F32),
            pltpu.VMEM((nd * 2, 8, LANES), F32),
            pltpu.VMEM((ndev, 8, LANES), F32),
            dma((3,)),
            dma((160,)),
            dma((160,)),
            dma((8,)),
            dma((ndev,)),
            dma((ndev,)),
            dma((nd * 2,)),
            dma((nd * 2,)),
            dma((ndev,)),
            dma((ndev,)),
        ],
        compiler_params=pltpu.CompilerParams(
            collective_id=0, has_side_effects=True, vmem_limit_bytes=67043328
        ),
    )(
        tokens,
        expert_of.reshape(micro, 1, toks),
        expert_of.reshape(micro, toks, 1),
        w_gate, w_up, w_down,
    )
    return out, scale[0, :experts]


def entry(tokens, expert_of, w_gate, w_up, w_down):
    micro, toks, width = tokens.shape
    ff = w_gate.shape[2]
    nd = lax.axis_size("dp")
    ne = lax.axis_size("expert")
    experts = ne // SPAN
    cap = max(2, 9 * toks // (8 * experts))
    extra = cap - ROWS
    fits = (
        micro == 2 and nd == 4 and experts == 4 and SPAN == 2 and extra > 0 and ROWS % extra == 0
        and (ne * extra) % ROWS == 0 and ff % LANES == 0 and (width * extra) % (ROWS * LANES * CHUNKS) == 0
    )
    if not fits:
        return body(tokens, expert_of, w_gate, w_up, w_down)
    return fused((micro, toks, width, ff, nd, ne, cap), tokens, expert_of, w_gate, w_up, w_down)


def solution(mesh):
    return jax.shard_map(
        entry,
        mesh=mesh,
        in_specs=(
            P(None, ("dp", "expert"), None),
            P(None, ("dp", "expert")),
            P("expert", None, "dp"),
            P("expert", None, "dp"),
            P("expert", "dp", None),
        ),
        out_specs=(P(None, ("dp", "expert"), None), P()),
        check_vma=False,
    )
```

```python
import functools

import jax
import jax.numpy as jnp
from jax import lax
from jax.experimental import pallas as pl
from jax.experimental.pallas import tpu as pltpu
from jax.sharding import PartitionSpec as P

SPAN = 2


clip_target = 2.0


def body(tokens, expert_of, w_gate, w_up, w_down):
    micro_count = tokens.shape[0]
    tok_rows = tokens.shape[1]
    model_width = tokens.shape[2]
    expert_size = lax.axis_size("expert")
    expert_count = expert_size // SPAN
    capacity = max(2, 9 * tok_rows // (8 * expert_count))
    my_expert = lax.axis_index("expert") // SPAN
    gate_local = w_gate[0]
    up_local = w_up[0]
    down_local = w_down[0]
    slot_range = jnp.arange(expert_count * capacity, dtype=jnp.int32)
    expert_range = jnp.arange(expert_count, dtype=jnp.int32)
    clip_scale = jnp.ones((expert_count,), jnp.float32)
    results = []
    for micro_idx in range(micro_count):
        token_ids = expert_of[micro_idx]
        onehot_ids = (token_ids[:, None] == expert_range[None, :]).astype(jnp.int32)
        earlier = jnp.cumsum(onehot_ids, axis=0) - onehot_ids
        slot_of = jnp.sum(earlier * onehot_ids, axis=1)
        position = token_ids * capacity + slot_of
        placing = (position[None, :] == slot_range[:, None]).astype(jnp.bfloat16)
        tokens_now = tokens[micro_idx]
        packed = jnp.dot(placing, tokens_now, preferred_element_type=jnp.float32).astype(
            jnp.bfloat16
        )
        packed = packed.reshape(expert_count, capacity, model_width)
        factor = clip_scale[my_expert]
        sending_all = jnp.repeat(packed, SPAN, axis=0)
        arrived = lax.all_to_all(sending_all, "expert", split_axis=0, concat_axis=0, tiled=True)
        flat_rows = arrived.reshape(expert_size * capacity, model_width)
        rows_in = lax.all_gather(flat_rows, "dp", axis=0, tiled=True)
        rows_in = (factor * rows_in.astype(jnp.float32)).astype(jnp.bfloat16)
        gate_vals = jnp.dot(rows_in, gate_local, preferred_element_type=jnp.float32)
        up_vals = jnp.dot(rows_in, up_local, preferred_element_type=jnp.float32)
        hidden = (jax.nn.silu(gate_vals) * up_vals).astype(jnp.bfloat16)
        summed = lax.psum_scatter(
            jnp.dot(hidden, down_local, preferred_element_type=jnp.float32).astype(jnp.bfloat16),
            "dp",
            scatter_dimension=0,
            tiled=True,
        )
        halves = summed.reshape(expert_size, capacity, model_width)
        returned = lax.all_to_all(halves, "expert", split_axis=0, concat_axis=0, tiled=True)
        returned = lax.optimization_barrier(returned)
        joined = jnp.sum(
            returned.reshape(expert_count, SPAN, capacity, model_width).astype(jnp.float32), axis=1
        )
        token_out = jnp.take(joined.reshape(expert_count * capacity, model_width), position, axis=0)
        results.append(token_out.astype(jnp.bfloat16))
        squares = jnp.sum(token_out * token_out, axis=1)
        onehot_float = onehot_ids.astype(jnp.float32)
        counts_local = jnp.sum(onehot_float, axis=0)
        square_local = jnp.dot(squares[None, :], onehot_float, precision=lax.Precision.HIGHEST)[0]
        counts, square_sums = lax.psum((counts_local, square_local), ("dp", "expert"))
        clip_scale = jnp.minimum(
            1.0,
            clip_target / jnp.sqrt((square_sums + model_width) / (model_width * (counts + 1.0))),
        )
    return (jnp.stack(results), clip_scale)


MESH = pl.DeviceIdType.MESH
F32 = jnp.float32
BF16 = jnp.bfloat16
ROWS = 16
CHUNKS = 4
LANES = 128


def mm(a, b):
    return jnp.dot(a, b, preferred_element_type=F32)


def iota(shape, dim):
    return lax.broadcasted_iota(jnp.int32, shape, dim)


def kernel(
    sizes,
    tok_ref, idr_ref, wg_hbm, wu_hbm, wd_hbm,
    out_ref, scale_ref,
    wg, wu, wd, pk, xg, xr, hid, g1, u1, sb, rb, own, rd, ra, rc, fr, f2, ret,
    cst, sqst, fst,
    wsem, ssem, rsem, lsem, csend, crecv, qsend, qrecv, fsend, frecv,
):
    micro, toks, width, ff, nd, ne, cap = sizes
    extra = cap - ROWS
    pieces = ROWS // extra
    piece = width // pieces
    experts = ne // SPAN
    blocks = experts * SPAN
    main_rows = blocks * ROWS
    extra_rows = blocks * extra
    half = width // 2
    ch = half // CHUNKS
    pair_w = 2 * ch
    pair_piece = pair_w // pieces
    ndev = nd * ne

    d = lax.axis_index("dp")
    ex = lax.axis_index("expert")
    z = ex // 2
    c = ex % 2
    dx = d + 1 - 2 * (d % 2)
    dy = d + 2 - 4 * (d // 2)
    dd = 3 - d
    sib = z * 2 + 1 - c
    flat = d * ne + ex
    flat_q = d * 2 + c

    weights = [
        pltpu.make_async_copy(wg_hbm.at[0], wg, wsem.at[0]),
        pltpu.make_async_copy(wu_hbm.at[0], wu, wsem.at[1]),
        pltpu.make_async_copy(wd_hbm.at[0], wd, wsem.at[2]),
    ]
    for copy in weights:
        copy.start()

    barrier = pltpu.get_barrier_semaphore()

    def greet(t, carry):
        to = (flat + t) % ndev
        pl.semaphore_signal(barrier, inc=1, device_id=(to // ne, to % ne), device_id_type=MESH)
        return carry

    lax.fori_loop(1, ndev, greet, 0)

    slots = experts * ROWS
    place = []
    counts = []
    for m in range(micro):
        idr = idr_ref[m]
        same = iota((toks, toks), 0) == iota((toks, toks), 1)
        idc = jnp.sum(jnp.where(same, idr, 0).astype(F32), axis=1, keepdims=True).astype(jnp.int32)
        before_r = (idc == idr) & (iota((toks, toks), 0) < iota((toks, toks), 1))
        slot_r = jnp.sum(before_r.astype(F32), axis=0, keepdims=True).astype(jnp.int32)
        before_c = (idc == idr) & (iota((toks, toks), 1) < iota((toks, toks), 0))
        slot_c = jnp.sum(before_c.astype(F32), axis=1, keepdims=True).astype(jnp.int32)
        place.append((idr, idc, slot_r, slot_c))
        hit = (idc == iota((toks, LANES), 1)).astype(F32)
        counts.append(jnp.sum(hit, axis=0, keepdims=True))
    row8 = iota((8, LANES), 0)
    lane8 = iota((8, LANES), 1)
    count_tile = jnp.zeros((8, LANES), F32)
    for m in range(micro):
        count_tile = jnp.where(row8 == m, counts[m], count_tile)
    cst[flat] = count_tile

    def pack(m):
        idr, _, slot_r, _ = place[m]
        row = iota((slots, toks), 0)
        pick = ((idr == row // ROWS) & (slot_r == row % ROWS)).astype(F32).astype(BF16)
        pick_x = ((idr == row // ROWS) & (slot_r == ROWS + (row % ROWS) // pieces)).astype(F32).astype(BF16)
        rowp = iota((slots, piece), 0) % pieces
        tail = jnp.zeros((slots, piece), F32)
        both = jnp.concatenate([pick, pick_x], axis=0)
        for p in range(pieces):
            got = mm(both, tok_ref[m, :, p * piece:(p + 1) * piece])
            pk[m, :, :, p * piece:(p + 1) * piece] = got[:slots].astype(BF16).reshape(experts, ROWS, piece)
            tail = jnp.where(rowp == p, got[slots:], tail)
        pk[m, :, :, width:] = tail.astype(BF16).reshape(experts, ROWS, piece)

    sends = []
    index = {}

    def sem_of(key):
        return index.setdefault(key, len(index))

    def remote(key, src, dst, dev):
        i = sem_of(key)
        copy = pltpu.make_async_remote_copy(
            src_ref=src, dst_ref=dst, send_sem=ssem.at[i], recv_sem=rsem.at[i],
            device_id=dev, device_id_type=MESH,
        )
        copy.start()
        sends.append((key, copy))
        return copy

    def arrived(key, dst):
        i = sem_of(key)
        pltpu.make_async_remote_copy(
            src_ref=dst, dst_ref=dst, send_sem=ssem.at[i], recv_sem=rsem.at[i],
            device_id=(d, sib), device_id_type=MESH,
        ).wait_recv()

    def wait_sent(match):
        left = []
        for key, copy in sends:
            if match(key):
                copy.wait_send()
            else:
                left.append((key, copy))
        sends[:] = left

    locals_ = {}

    def local(key, src, dst):
        i = len(locals_)
        copy = pltpu.make_async_copy(src, dst, lsem.at[i])
        copy.start()
        locals_[key] = copy

    def zof(t):
        return (z + experts - t) % experts

    def dispatch(m):
        local(("z", m), pk.at[m, z], xg.at[m, d, c * experts + z])
        for t in range(1, experts):
            to = (z + t) % experts
            remote(("z", m, t), pk.at[m, to], xg.at[m, d, c * experts + z], (d, to * 2 + c))

    def to_sibling(kind, m, t, slot):
        remote(("s" + kind, m, t), slot, slot, (d, sib))

    def gather_own(m, t):
        slot = xg.at[m, d, c * experts + zof(t)]
        if t == 0:
            locals_[("z", m)].wait()
        else:
            arrived(("z", m, t), slot)
        remote(("gx", m, t), slot, slot, (dx, ex))
        remote(("gy", m, t), slot, slot, (dy, ex))
        to_sibling("o", m, t, slot)

    def gather_xy(m, t):
        slot = xg.at[m, dx, c * experts + zof(t)]
        arrived(("gx", m, t), slot)
        if t < experts // 2:
            remote(("gd", m, t), slot, slot, (dy, ex))
        to_sibling("x", m, t, slot)
        slot = xg.at[m, dy, c * experts + zof(t)]
        arrived(("gy", m, t), slot)
        if t >= experts // 2:
            remote(("gd", m, t), slot, slot, (dx, ex))
        to_sibling("y", m, t, slot)

    def gather_diag(m, t):
        slot = xg.at[m, dd, c * experts + zof(t)]
        arrived(("gd", m, t), slot)
        to_sibling("d", m, t, slot)

    def gather_end(m):
        for kind, chip in (("o", d), ("x", dx), ("y", dy), ("d", dd)):
            for t in range(experts):
                arrived(("s" + kind, m, t), xg.at[m, chip, (1 - c) * experts + zof(t)])

    allm = nd * main_rows
    allx = nd * extra_rows

    def spread(m):
        def one(p, carry):
            row = iota((allx, allm), 0)
            want = (row // extra) * ROWS + (row % extra) * pieces + p
            pick = (iota((allx, allm), 1) == want).astype(F32).astype(BF16)
            tails = xg[m, :, :, :, width:].reshape(allm, piece)
            xr[:, pl.ds(pl.multiple_of(p * piece, piece), piece)] = mm(pick, tails).astype(BF16)
            return carry

        lax.fori_loop(0, pieces, one, 0)

    def gate_up(m, low, high):
        def one(n, carry):
            cols = pl.ds(pl.multiple_of(n * LANES, LANES), LANES)
            rows = jnp.concatenate([xg[m, :, :, :, :width].reshape(allm, width), xr[...]], axis=0)
            w = jnp.concatenate([wg[:, cols], wu[:, cols]], axis=1)
            both = mm(rows, w)
            gate = both[:, :LANES]
            up = both[:, LANES:]
            if m == 0:
                hid[:, cols] = (gate / (1.0 + jnp.exp(-gate)) * up).astype(BF16)
            else:
                g1[:, cols] = gate
                u1[:, cols] = up
            return carry

        lax.fori_loop(low, high, one, 0)

    def scaled_hidden(scale):
        def one(n, carry):
            cols = pl.ds(pl.multiple_of(n * LANES, LANES), LANES)
            gate = g1[:, cols] * scale
            up = u1[:, cols] * scale
            hid[:, cols] = (gate / (1.0 + jnp.exp(-gate)) * up).astype(BF16)
            return carry

        lax.fori_loop(0, ff // LANES, one, 0)

    def neighbours(j):
        return (dx, dy) if j % 2 == 0 else (dy, dx)

    def down(side, j):
        col = pl.multiple_of(side * half + j * ch, ch)
        return mm(hid[...], wd[:, pl.ds(col, ch)])

    def step_a(m, j):
        if m > 0:
            wait_sent(lambda key: key == ("rs", m - 1, j))
        sb[j] = down(1 - c, j).astype(BF16)
        remote(("rs", m, j), sb.at[j], rb.at[m, j], (d, sib))

    def step_b(m, j):
        mine = down(c, j)
        if m > 0:
            wait_sent(lambda key: key[0] in ("rd", "ra", "rc") and key[1:] == (m - 1, j))
        arrived(("rs", m, j), rb.at[m, j])
        both = (mine + rb[m, j].astype(F32)).astype(BF16)
        for k in range(nd):
            own[j, k, :main_rows] = both[k * main_rows:(k + 1) * main_rows]
            own[j, k, main_rows:] = both[allm + k * extra_rows:allm + (k + 1) * extra_rows]
        first, _ = neighbours(j)
        remote(("rd", m, j), own.at[j, dd], rd.at[m, j], (first, ex))
        remote(("ra", m, j), own.at[j, first], ra.at[m, j], (first, ex))

    def step_c(m, j):
        _, second = neighbours(j)
        arrived(("rd", m, j), rd.at[m, j])
        own[j, second] = (own[j, second].astype(F32) + rd[m, j].astype(F32)).astype(BF16)
        remote(("rc", m, j), own.at[j, second], rc.at[m, j], (second, ex))

    def span(j):
        return (0, ch) if j % 2 == 0 else (ch, pair_w + pair_piece)

    def step_d(m, j):
        arrived(("ra", m, j), ra.at[m, j])
        arrived(("rc", m, j), rc.at[m, j])
        total = own[j, d].astype(F32) + ra[m, j].astype(F32) + rc[m, j].astype(F32)
        at = (j % 2) * ch
        pair = j // 2
        low = total.astype(BF16)
        f2[m, pair, :, :, at:at + ch] = low[:main_rows].reshape(blocks, ROWS, ch)
        fr[:, at:at + ch] = low[main_rows:]
        if j % 2 == 1:
            row = iota((main_rows, extra_rows), 0)
            want = (row // ROWS) * extra + (row % ROWS) // pieces
            pick = (iota((main_rows, extra_rows), 1) == want).astype(F32).astype(BF16)
            rowp = iota((main_rows, pair_piece), 0) % pieces
            tail = jnp.zeros((main_rows, pair_piece), F32)
            for p in range(pieces):
                tail = jnp.where(rowp == p, mm(pick, fr[:, p * pair_piece:(p + 1) * pair_piece]), tail)
            f2[m, pair, :, :, pair_w:] = tail.astype(BF16).reshape(blocks, ROWS, pair_piece)
        low_col, high_col = span(j)
        local(
            ("f", m, j), f2.at[m, pair, c * experts + z, :, low_col:high_col],
            ret.at[m, z, c, pair, :, low_col:high_col],
        )
        for t in range(1, blocks):
            to = (ex + t) % blocks
            remote(
                ("f", m, j, t), f2.at[m, pair, (to % 2) * experts + to // 2, :, low_col:high_col],
                ret.at[m, z, c, pair, :, low_col:high_col], (d, to),
            )
        return jnp.sum(jnp.sum(total * total, axis=0, keepdims=True), axis=1, keepdims=True)

    def unpack(m):
        _, idc, _, slot_c = place[m]
        col = iota((toks, slots), 1)
        pick = ((idc == col // ROWS) & (slot_c == col % ROWS)).astype(F32).astype(BF16)
        pick_x = (idc == col // ROWS) & (slot_c == ROWS + (col % ROWS) // pieces)
        picks = jnp.concatenate(
            [(pick_x & (col % pieces == p)).astype(F32).astype(BF16) for p in range(pieces)], axis=0
        )
        for j in range(CHUNKS):
            locals_[("f", m, j)].wait()
            low, high = span(j)
            for t in range(1, blocks):
                frm = (ex + blocks - t) % blocks
                arrived(("f", m, j, t), ret.at[m, frm // 2, frm % 2, j // 2, :, low:high])
        for h in range(2):
            for pair in range(CHUNKS // 2):
                main = mm(pick, ret[m, :, h, pair, :, :pair_w].reshape(slots, pair_w))
                tails = mm(picks, ret[m, :, h, pair, :, pair_w:].reshape(slots, pair_piece))
                for p in range(pieces):
                    at = p * pair_piece
                    value = main[:, at:at + pair_piece] + tails[p * toks:(p + 1) * toks]
                    base = h * half + pair * pair_w + at
                    out_ref[m, :, base:base + pair_piece] = value.astype(BF16)

    def clip(total, count):
        return jnp.minimum(1.0, clip_target / jnp.sqrt((total + width) / (width * (count + 1.0))))

    pack(0)
    pl.semaphore_wait(barrier, ndev - 1)
    dispatch(0)

    def spread_stats(buf, me, peers, ssems, rsems, dev_of):
        def one(t, carry):
            pltpu.make_async_remote_copy(
                src_ref=buf.at[me], dst_ref=buf.at[me], send_sem=ssems.at[t], recv_sem=rsems.at[t],
                device_id=dev_of((me + t) % peers), device_id_type=MESH,
            ).start()
            return carry

        lax.fori_loop(1, peers, one, 0)

    def await_stats(buf, me, peers, ssems, rsems, dev_of):
        def one(t, carry):
            frm = (me + peers - t) % peers
            copy = pltpu.make_async_remote_copy(
                src_ref=buf.at[me], dst_ref=buf.at[frm], send_sem=ssems.at[t], recv_sem=rsems.at[t],
                device_id=dev_of((me + t) % peers), device_id_type=MESH,
            )
            copy.wait_recv()
            copy.wait_send()
            return carry

        lax.fori_loop(1, peers, one, 0)

    whole = (ndev, csend, crecv, lambda g: (g // ne, g % ne))
    plane = (nd * 2, qsend, qrecv, lambda q: (q // 2, z * 2 + q % 2))
    last = (ndev, fsend, frecv, lambda g: (g // ne, g % ne))

    spread_stats(cst, flat, *whole)
    gather_own(0, 0)
    pack(1)
    for t in range(1, experts):
        gather_own(0, t)
        if t > 1:
            gather_xy(0, t - 2)
    dispatch(1)
    for t in range(experts - 2, experts):
        gather_xy(0, t)
    gather_own(1, 0)
    for t in range(experts):
        gather_diag(0, t)
    gather_end(0)
    weights[0].wait()
    weights[1].wait()
    tiles = ff // LANES
    marks = [0, (2 * tiles) // 7, (4 * tiles) // 7, tiles]
    spread(0)
    gather_own(1, 1)
    gate_up(0, marks[0], marks[1])
    for t in range(2, experts):
        gather_own(1, t)
    gate_up(0, marks[1], marks[2])
    for t in range(experts // 2):
        gather_xy(1, t)
    gate_up(0, marks[2], marks[3])
    weights[2].wait()
    step_a(0, 0)
    step_a(0, 1)
    step_b(0, 0)
    for t in range(experts // 2, experts):
        gather_xy(1, t)
    step_a(0, 2)
    step_b(0, 1)
    step_a(0, 3)
    step_b(0, 2)
    step_b(0, 3)
    for t in range(experts):
        gather_diag(1, t)
    step_c(0, 0)
    gather_end(1)
    spread(1)
    step_c(0, 1)
    gate_up(1, marks[0], marks[1])
    step_c(0, 2)
    gate_up(1, marks[1], marks[2])
    step_c(0, 3)
    squares = step_d(0, 0)
    squares = squares + step_d(0, 1)
    gate_up(1, marks[2], marks[3])
    squares = squares + step_d(0, 2)
    squares = squares + step_d(0, 3)
    sqst[flat_q] = jnp.broadcast_to(squares, (8, LANES))
    spread_stats(sqst, flat_q, *plane)
    await_stats(cst, flat, *whole)
    count_sum = jnp.sum(cst[...], axis=0)
    await_stats(sqst, flat_q, *plane)
    square_sum = jnp.sum(sqst[...], axis=0)[:1, :1]
    masked = jnp.where((row8 == 0) & (lane8 == z), count_sum, 0.0)
    count_here = jnp.sum(jnp.sum(masked, axis=0, keepdims=True), axis=1, keepdims=True)
    scaled_hidden(clip(square_sum, count_here))
    step_a(1, 0)
    step_a(1, 1)
    step_b(1, 0)
    step_a(1, 2)
    step_b(1, 1)
    step_c(1, 0)
    step_a(1, 3)
    step_b(1, 2)
    step_c(1, 1)
    step_b(1, 3)
    step_c(1, 2)
    squares = step_d(1, 0)
    step_c(1, 3)
    squares = squares + step_d(1, 1)
    unpack(0)
    squares = squares + step_d(1, 2)
    squares = squares + step_d(1, 3)
    fst[flat] = jnp.where(lane8 == z, jnp.broadcast_to(squares, (8, LANES)), 0.0)
    spread_stats(fst, flat, *last)
    unpack(1)
    await_stats(fst, flat, *last)
    count_last = jnp.sum(jnp.where(row8 == micro - 1, count_sum, 0.0), axis=0, keepdims=True)
    scale_ref[...] = clip(jnp.sum(fst[...], axis=0), count_last)
    wait_sent(lambda key: True)


def fused(sizes, tokens, expert_of, w_gate, w_up, w_down):
    micro, toks, width, ff, nd, ne, cap = sizes
    extra = cap - ROWS
    pieces = ROWS // extra
    piece = width // pieces
    experts = ne // SPAN
    blocks = experts * SPAN
    ch = width // 2 // CHUNKS
    wide = width + piece
    pair_wide = 2 * ch + 2 * ch // pieces
    rows = nd * blocks * cap
    one = blocks * cap
    ndev = nd * ne
    dma = pltpu.SemaphoreType.DMA
    vmem = pl.BlockSpec(memory_space=pltpu.VMEM)
    anyw = pl.BlockSpec(memory_space=pl.ANY)
    out, scale = pl.pallas_call(
        functools.partial(kernel, sizes),
        out_shape=(
            jax.ShapeDtypeStruct((micro, toks, width), BF16),
            jax.ShapeDtypeStruct((8, LANES), F32),
        ),
        in_specs=[vmem, vmem, anyw, anyw, anyw],
        out_specs=(vmem, vmem),
        scratch_shapes=[
            pltpu.VMEM((width, ff), BF16),
            pltpu.VMEM((width, ff), BF16),
            pltpu.VMEM((ff, width), BF16),
            pltpu.VMEM((micro, experts, ROWS, wide), BF16),
            pltpu.VMEM((micro, nd, blocks, ROWS, wide), BF16),
            pltpu.VMEM((nd * blocks * extra, width), BF16),
            pltpu.VMEM((rows, ff), BF16),
            pltpu.VMEM((rows, ff), F32),
            pltpu.VMEM((rows, ff), F32),
            pltpu.VMEM((CHUNKS, rows, ch), BF16),
            pltpu.VMEM((micro, CHUNKS, rows, ch), BF16),
            pltpu.VMEM((CHUNKS, nd, one, ch), BF16),
            pltpu.VMEM((micro, CHUNKS, one, ch), BF16),
            pltpu.VMEM((micro, CHUNKS, one, ch), BF16),
            pltpu.VMEM((micro, CHUNKS, one, ch), BF16),
            pltpu.VMEM((blocks * extra, 2 * ch), BF16),
            pltpu.VMEM((micro, CHUNKS // 2, blocks, ROWS, pair_wide), BF16),
            pltpu.VMEM((micro, experts, 2, CHUNKS // 2, ROWS, pair_wide), BF16),
            pltpu.VMEM((ndev, 8, LANES), F32),
            pltpu.VMEM((nd * 2, 8, LANES), F32),
            pltpu.VMEM((ndev, 8, LANES), F32),
            dma((3,)),
            dma((224,)),
            dma((224,)),
            dma((16,)),
            dma((ndev,)),
            dma((ndev,)),
            dma((nd * 2,)),
            dma((nd * 2,)),
            dma((ndev,)),
            dma((ndev,)),
        ],
        compiler_params=pltpu.CompilerParams(
            collective_id=0, has_side_effects=True, vmem_limit_bytes=67043328
        ),
    )(
        tokens,
        expert_of.reshape(micro, 1, toks),
        w_gate, w_up, w_down,
    )
    return out, scale[0, :experts]


def entry(tokens, expert_of, w_gate, w_up, w_down):
    micro, toks, width = tokens.shape
    ff = w_gate.shape[2]
    nd = lax.axis_size("dp")
    ne = lax.axis_size("expert")
    experts = ne // SPAN
    cap = max(2, 9 * toks // (8 * experts))
    extra = cap - ROWS
    fits = (
        micro == 2 and nd == 4 and experts == 4 and SPAN == 2 and extra > 0 and ROWS % extra == 0
        and (ne * extra) % ROWS == 0 and ff % LANES == 0 and (width * extra) % (ROWS * LANES * CHUNKS) == 0
    )
    if not fits:
        return body(tokens, expert_of, w_gate, w_up, w_down)
    return fused((micro, toks, width, ff, nd, ne, cap), tokens, expert_of, w_gate, w_up, w_down)


def solution(mesh):
    return jax.shard_map(
        entry,
        mesh=mesh,
        in_specs=(
            P(None, ("dp", "expert"), None),
            P(None, ("dp", "expert")),
            P("expert", None, "dp"),
            P("expert", None, "dp"),
            P("expert", "dp", None),
        ),
        out_specs=(P(None, ("dp", "expert"), None), P()),
        check_vma=False,
    )
```
